32 devices in a mesh: fsdp: 8 (over z, x), seq: 4 (over y, core).
Axes of the slice: x: 2, y: 2, z: 4, core: 2. Of those that a mesh axis runs over, the one named last changes fastest.
Arguments:
- context: bfloat16 [16, 512, 2560], P('fsdp', 'seq'), may hold values from -6 to 6
- residual: bfloat16 [16, 512, 2560], P('fsdp', 'seq'), may hold values from -6 to 6
- target_rows: bfloat16 [16, 512, 2560], P('fsdp', 'seq'), may hold values from -0.00390625 to 0.00390625
- log_norm: float32 [16, 512], P('fsdp', 'seq'), may hold values from -0.15 to 0.15
- norm_gain: float32 [2560], replicated, may hold values from 0.1 to 1.9
- out_proj: bfloat16 [2560, 2560], P('fsdp'), may hold values from -0.125 to 0.125
- old_logprob: float32 [16, 512], P('fsdp', 'seq'), may hold values from -0.15 to 0.15
- lengths: int32 [16, 4], P('fsdp', 'seq'), may hold values from 112 to 128
- rewards: float32 [16, 4], P('fsdp', 'seq'), may hold values from -5 to 5
- prompt_ids: int32 [16, 4], P('fsdp', 'seq'), may hold values from 0 to 3, as said below
- placement: int32 [16, 4], P('fsdp', 'seq'), may hold values from 0 to 15, as said below
Outputs:
- grad_context: bfloat16 [16, 512, 2560], P('fsdp', 'seq')
- grad_weight: float32 [2560, 2560], P('fsdp')
- loss: float32 [], replicated
The draws below stay inside these ranges and needn't reach their ends.
Inputs may be any that keep to these rules, and one draw needn't show every extreme that they name: `prompt_ids`: every prompt id names exactly 16 rows. Sampler row (a, s) goes to learner row (placement[a, s], s) and keeps a mod 2; the 2 rows of one device go to 2 different fsdp indices; every learner row receives exactly one row; in every column one of the 2 rows of each device goes 8 / 2 fsdp indices onward and another goes 1 index onward, counted round.
All inputs are finite; a program needn't handle non-finite values.
Results may differ from the reference program's by a relative error of at most 0.014.
Values may be sent and summed in bfloat16 or wider, within the bound.
A program may use at most 128 MiB of HBM per device.

```python
import math
import jax
import jax.numpy as jnp
from jax import lax

DW = 2560
AW = 2560
RS = 2
LMAX = 128
GS = 16
FSDP_WAYS = 8
SEQ_WAYS = 4
FROWS = 16
POSITIONS = 512
ROWS_ALL = 64
PROMPTS = 4
ALL_TOKENS = 8192


def draw_prompt_ids(key, part):
    order = jax.random.permutation(key, ROWS_ALL)
    return (order // GS).astype(jnp.int32).reshape(FROWS, SEQ_WAYS)


def pick_shifts(subkey):
    first_key, second_key = jax.random.split(subkey)
    halfway = FSDP_WAYS // 2
    others = jax.random.permutation(first_key, FSDP_WAYS - 2).astype(jnp.int32)
    others = jnp.where(others >= 1, others + 1, others)
    others = jnp.where(others >= halfway, others + 1, others)
    chosen = jnp.concatenate([jnp.full((1,), halfway, jnp.int32), jnp.ones((1,), jnp.int32), others[:RS - 2]])
    return chosen[jax.random.permutation(second_key, RS)]


def draw_placement(key, part):
    subkeys = jax.random.split(jax.random.fold_in(key, 7), SEQ_WAYS)
    shifts = jax.vmap(pick_shifts)(subkeys)
    row_index = jnp.arange(FROWS, dtype=jnp.int32)
    owner = row_index // RS
    within = row_index % RS
    moved = shifts.T[within]
    target = (owner[:, None] + moved) % FSDP_WAYS
    return (target * RS + within[:, None]).astype(jnp.int32)


def place_ends(drawn, key, low, largest):
    place = [jax.random.randint(jax.random.fold_in(key, axis), (), 0, length) for axis, length in enumerate(drawn.shape)]
    longest = drawn.shape.index(max(drawn.shape))
    next_to = place[:longest] + [(place[longest] + 1) % drawn.shape[longest]] + place[longest + 1:]
    return drawn.at[tuple(place)].set(low).at[tuple(next_to)].set(largest)


def block_scale(rng, dims, cuts, least, high):
    gain, own = 1.0, jax.random.fold_in(rng, 6)
    for position, shards_of in cuts:
        heights = jnp.exp(jax.random.uniform(jax.random.fold_in(own, position), (shards_of,), jnp.float32, least / len(cuts), high / len(cuts)))
        gain = gain * jnp.repeat(heights, dims[position] // shards_of).reshape([-1 if axis == position else 1 for axis in range(len(dims))])
    return gain


def normal_values(own_key, extent, spread, bound, shards=(), kind=jnp.bfloat16):
    entries = jax.random.normal(own_key, extent, jnp.float32) * spread
    if len(shards) > 0:
        entries = block_scale(own_key, extent, shards, -0.22, 0.18) * entries
    return jnp.clip(entries, min=-bound, max=bound).astype(kind)


def setup_inputs(seed: int = 0) -> dict:
    splits = jax.random.split(jax.random.key(seed), 12)
    context = normal_values(splits[0], (FROWS, POSITIONS, AW), 1.0, 6.0, ((0, 8), (1, 4)))
    residual = normal_values(splits[1], (FROWS, POSITIONS, DW), 1.0, 6.0, ((0, 8), (1, 4)))
    target_rows = normal_values(splits[2], (FROWS, POSITIONS, DW), (1024 * DW) ** -0.5, 0.00390625, ((0, 8), (1, 4)))
    log_norm = normal_values(splits[3], (FROWS, POSITIONS), 0.05, 0.15, ((0, 8), (1, 4)), jnp.float32)
    norm_gain = jnp.clip(1.0 + 0.18 * jax.random.normal(splits[4], (DW,), jnp.float32), 0.1, 1.9)
    out_proj = normal_values(splits[5], (AW, DW), AW ** -0.5, 0.125, ((0, 8),))
    old_logprob = normal_values(splits[6], (FROWS, POSITIONS), 0.05, 0.15, ((0, 8), (1, 4)), jnp.float32)
    lengths = place_ends(jax.random.randint(splits[7], (FROWS, SEQ_WAYS), LMAX - LMAX // 8, LMAX + 1), jax.random.fold_in(splits[7], 1), LMAX - LMAX // 8, LMAX).astype(jnp.int32)
    rewards = normal_values(splits[8], (FROWS, SEQ_WAYS), 1.0, 5.0, ((0, 8), (1, 4)), jnp.float32)
    prompt_ids = draw_prompt_ids(jax.random.fold_in(splits[11], 71), 0)
    placement = draw_placement(jax.random.fold_in(splits[11], 71), 0)
    return dict(context=context, residual=residual, target_rows=target_rows, log_norm=log_norm, norm_gain=norm_gain, out_proj=out_proj, old_logprob=old_logprob, lengths=lengths, rewards=rewards, prompt_ids=prompt_ids, placement=placement)


def reference(context, residual, target_rows, log_norm, norm_gain, out_proj, old_logprob, lengths, rewards, prompt_ids, placement):
    reward_flat = rewards.reshape(-1)
    prompt_flat = prompt_ids.reshape(-1)
    onehot = (prompt_flat[:, None] == jnp.arange(PROMPTS, dtype=jnp.int32)[None, :]).astype(jnp.float32)
    group_sum = lax.optimization_barrier(jnp.sum(onehot * reward_flat[:, None], axis=0))
    group_sq = lax.optimization_barrier(jnp.sum(onehot * (reward_flat * reward_flat)[:, None], axis=0))
    count = jnp.sum(lengths.astype(jnp.float32))
    group_mean = group_sum / GS
    group_var = group_sq / GS - group_mean * group_mean
    row_mean = lax.optimization_barrier(jnp.sum(onehot * group_mean[None, :], axis=1))
    row_var = lax.optimization_barrier(jnp.sum(onehot * group_var[None, :], axis=1))
    advantage = ((reward_flat - row_mean) / jnp.sqrt(row_var + 0.25)).reshape(FROWS, SEQ_WAYS)
    column = jnp.broadcast_to(jnp.arange(SEQ_WAYS, dtype=jnp.int32)[None, :], (FROWS, SEQ_WAYS))
    learn_adv = jnp.zeros((FROWS, SEQ_WAYS), jnp.float32).at[placement, column].set(advantage)
    learn_len = jnp.zeros((FROWS, SEQ_WAYS), jnp.int32).at[placement, column].set(lengths)
    old_blocks = old_logprob.reshape(FROWS, SEQ_WAYS, LMAX)
    learn_old = jnp.zeros((FROWS, SEQ_WAYS, LMAX), jnp.float32).at[placement, column].set(old_blocks)
    offsets = jnp.arange(LMAX, dtype=jnp.int32)
    valid = (offsets[None, None, :] < learn_len[:, :, None]).astype(jnp.float32).reshape(-1)
    token_adv = jnp.broadcast_to(learn_adv[:, :, None], (FROWS, SEQ_WAYS, LMAX)).reshape(-1)
    context_flat = context.reshape(-1, AW)
    hidden = residual.reshape(-1, DW).astype(jnp.float32) + jnp.dot(context_flat, out_proj, preferred_element_type=jnp.float32)
    rinv = lax.rsqrt(lax.optimization_barrier(jnp.mean(hidden * hidden, axis=1)) + 1e-06)
    vecs = norm_gain[None, :] * target_rows.reshape(-1, DW).astype(jnp.float32)
    hv_sum = lax.optimization_barrier(jnp.sum(hidden * vecs, axis=1))
    score = hv_sum * rinv
    ratio = jnp.exp(score - log_norm.reshape(-1) - learn_old.reshape(-1))
    plain = ratio * token_adv
    clipped = jnp.clip(ratio, 0.8, 1.2) * token_adv
    objective = jnp.minimum(plain, clipped)
    loss = jnp.sum(valid * -objective) / count
    dscore = -valid * jnp.where(plain <= clipped, plain, 0.0) / count
    dhid = (dscore * rinv)[:, None] * (vecs - hidden * (rinv * rinv * hv_sum / DW)[:, None])
    grad_hidden = (dhid * (32.0 * ALL_TOKENS * math.sqrt(DW))).astype(jnp.bfloat16)
    grad_context = jnp.dot(grad_hidden, out_proj.T, preferred_element_type=jnp.float32).astype(jnp.bfloat16)
    grad_context = grad_context.reshape(FROWS, POSITIONS, AW)
    ctx_dev = context.reshape(FSDP_WAYS, RS, SEQ_WAYS, LMAX, AW).transpose(0, 2, 1, 3, 4).reshape(FSDP_WAYS * SEQ_WAYS, RS * LMAX, AW)
    grad_dev = grad_hidden.reshape(FSDP_WAYS, RS, SEQ_WAYS, LMAX, DW).transpose(0, 2, 1, 3, 4).reshape(FSDP_WAYS * SEQ_WAYS, RS * LMAX, DW)

    def add_device(total, pieces):
        term = lax.dot_general(pieces[0], pieces[1], (((0,), (0,)), ((), ())), preferred_element_type=jnp.float32)
        term = lax.optimization_barrier(term.astype(jnp.bfloat16))
        return (total + term.astype(jnp.float32), None)
    total, unused = lax.scan(add_device, jnp.zeros((AW, DW), jnp.float32), (ctx_dev, grad_dev))
    grad_weight = total * (1.0 / math.sqrt(ALL_TOKENS))
    return (grad_context, grad_weight, loss)
```

```python
import functools
import math

import jax
import jax.numpy as jnp
from jax import lax
from jax.experimental import pallas as pl
from jax.experimental.pallas import tpu as pltpu
from jax.sharding import PartitionSpec as P

GS = 16
FO = 4
Q = 4
MESH = pl.DeviceIdType.MESH
F32 = jnp.float32
BF16 = jnp.bfloat16


def kernel(
    dims,
    ctx,
    res,
    tgt,
    lognorm,
    gain,
    wown,
    packet,
    gctx,
    gw,
    loss_out,
    w,
    ctxt,
    hid,
    ghs,
    ghr,
    dws,
    irecv,
    part,
    obuf,
    orecv,
    fsend,
    frecv,
    pk,
    ls,
    ag_o,
    ag_i,
    ag_c,
    cx,
    gx,
    rs_i,
    rs_o,
    fin,
    pk1,
    pk2,
    pk3,
    ls1,
    ls2,
    ls3,
):
    fsdp_ways, seq_ways, nrows, lmax, dw, aw = dims
    fi = fsdp_ways // FO
    so_ways = seq_ways // Q
    tokens = nrows * lmax
    blk = aw // fsdp_ways
    cq = dw // Q
    prompts = nrows * fsdp_ways * seq_ways // GS
    prows = max(8, prompts)
    all_tokens = tokens * fsdp_ways * seq_ways
    f = lax.axis_index("fsdp")
    s = lax.axis_index("seq")
    o = f // fi
    i = lax.rem(f, fi)
    so = s // Q
    q = lax.rem(s, Q)
    c = lax.rem(q, 2)

    def outer_dev(k, m=0):
        return (lax.rem(o + k, FO) * fi + i, lax.rem(so + m, so_ways) * Q + q)

    def inner_dev(j):
        return (o * fi + lax.rem(i + j, fi), s)

    def group_dev(k):
        return (f, so * Q + lax.rem(q + k, Q))

    core_dev = (f, so * Q + q + 1 - 2 * c)
    outer = [(m, k) for k in range(FO) for m in range(so_ways) if (m, k) != (0, 0)]
    barrier = pltpu.get_barrier_semaphore()
    peers = [outer_dev(k, m) for m, k in outer]
    peers += [inner_dev(j) for j in range(1, fi)]
    peers += [group_dev(k) for k in range(1, Q)]
    for peer in peers:
        pl.semaphore_signal(barrier, inc=1, device_id=peer, device_id_type=MESH)
    pl.semaphore_wait(barrier, len(peers))

    sent = []

    def send(src, dst, sems, index, dev):
        copy = pltpu.make_async_remote_copy(
            src_ref=src,
            dst_ref=dst,
            send_sem=sems.at[(0,) + index],
            recv_sem=sems.at[(1,) + index],
            device_id=dev,
            device_id_type=MESH,
        )
        copy.start()
        sent.append(copy)

    def arrive(dst, sems, index, dev):
        pltpu.make_async_remote_copy(
            src_ref=dst,
            dst_ref=dst,
            send_sem=sems.at[(0,) + index],
            recv_sem=sems.at[(1,) + index],
            device_id=dev,
            device_id_type=MESH,
        ).wait_recv()

    def rows_of(owner):
        return pl.ds(pl.multiple_of(owner * blk, blk), blk)

    def half(owner, side):
        return w.at[pl.ds(2 * side, 2), rows_of(owner), :]

    pk[o, so, i, q] = packet[...]
    for k in range(1, Q):
        mine = pk.at[o, so, i, q]
        send(mine, mine, pk1, (k,), group_dev(k))

    for part_q in range(Q):
        w[part_q, rows_of(f), :] = wown[:, part_q * cq : (part_q + 1) * cq]
    for k in (2, 1, 3):
        send(half(f, c), half(f, c), ag_o, (k,), outer_dev(k))
    for j in range(1, fi):
        send(half(f, c), half(f, c), ag_i, (0, j), inner_dev(j))

    @pl.loop(0, aw // 256)
    def _(t):
        span = pl.ds(pl.multiple_of(t * 256, 256), 256)
        ctxt[q, span, :] = ctx[:, span].T

    for k in range(1, Q):
        send(ctxt.at[q], ctxt.at[q], cx, (k,), group_dev(k))

    for k in range(1, Q):
        there = pk.at[o, so, i, lax.rem(q + Q - k, Q)]
        arrive(there, pk1, (k,), group_dev(k))
    for j in range(1, fi):
        mine = pk.at[o, so, i]
        send(mine, mine, pk2, (j,), inner_dev(j))
    for j in range(1, fi):
        there = pk.at[o, so, lax.rem(i + fi - j, fi)]
        arrive(there, pk2, (j,), inner_dev(j))
    for m, k in outer:
        mine = pk.at[o, so]
        send(mine, mine, pk3, (m, k), outer_dev(k, m))
    for m, k in outer:
        there = pk.at[lax.rem(o + FO - k, FO), lax.rem(so + so_ways - m, so_ways)]
        arrive(there, pk3, (m, k), outer_dev(k, m))

    prompt_row = lax.broadcasted_iota(jnp.int32, (prows, 128), 0).astype(F32)
    zero_p = jnp.zeros((prows, 128), F32)
    zero_r = jnp.zeros((1, 128), F32)

    def over_devices(fa, carry):
        for sa in range(seq_ways):
            at = (fa // fi, sa // Q, lax.rem(fa, fi), sa % Q)
            for r in range(nrows):
                gsum, gsq, count = carry
                reward = pk[at + (pl.ds(nrows + r, 1), slice(None))]
                prompt = pk[at + (pl.ds(2 * nrows + r, 1), slice(None))]
                length = pk[at + (pl.ds(3 * nrows + r, 1), slice(None))]
                hot = prompt == prompt_row
                gsum = gsum + jnp.where(hot, reward, 0.0)
                gsq = gsq + jnp.where(hot, reward * reward, 0.0)
                carry = (gsum, gsq, count + length)
        return carry

    gsum, gsq, count = lax.fori_loop(0, fsdp_ways, over_devices, (zero_p, zero_p, zero_r))
    gmean = gsum / GS
    gvar = gsq / GS - gmean * gmean

    def over_column(fa, carry):
        at = (fa // fi, so, lax.rem(fa, fi), q)
        for r in range(nrows):
            old = pk[at + (pl.ds(r, 1), slice(None))]
            reward = pk[at + (pl.ds(nrows + r, 1), slice(None))]
            prompt = pk[at + (pl.ds(2 * nrows + r, 1), slice(None))]
            length = pk[at + (pl.ds(3 * nrows + r, 1), slice(None))]
            dest = pk[at + (pl.ds(4 * nrows + r, 1), slice(None))]
            hot = prompt == prompt_row
            mean = jnp.sum(jnp.where(hot, gmean, 0.0), axis=0, keepdims=True)
            var = jnp.sum(jnp.where(hot, gvar, 0.0), axis=0, keepdims=True)
            adv = (reward - mean) / jnp.sqrt(var + 0.25)
            fresh = []
            for j in range(nrows):
                chosen = dest == (f * nrows + j).astype(F32)
                l_old, l_adv, l_len = carry[3 * j : 3 * j + 3]
                fresh += [
                    l_old + jnp.where(chosen, old, 0.0),
                    l_adv + jnp.where(chosen, adv, 0.0),
                    l_len + jnp.where(chosen, length, 0.0),
                ]
            carry = tuple(fresh)
        return carry

    learned = lax.fori_loop(0, fsdp_ways, over_column, (zero_r,) * (3 * nrows))
    eye_r = lax.broadcasted_iota(jnp.int32, (lmax, lmax), 0)
    eye_c = lax.broadcasted_iota(jnp.int32, (lmax, lmax), 1)
    offset = lax.broadcasted_iota(jnp.int32, (lmax, 1), 0).astype(F32)

    def upright(row):
        spread = jnp.broadcast_to(row, (lmax, lmax))
        return jnp.sum(jnp.where(eye_r == eye_c, spread, 0.0), axis=1, keepdims=True)

    base, token_adv, valid = [], [], []
    for j in range(nrows):
        l_old, l_adv, l_len = learned[3 * j : 3 * j + 3]
        base.append(upright(lognorm[pl.ds(j, 1), :]) + upright(l_old))
        token_adv.append(jnp.broadcast_to(l_adv[:, 0:1], (lmax, 1)))
        valid.append((offset < l_len[:, 0:1]).astype(F32))
    base = jnp.concatenate(base, axis=0)
    token_adv = jnp.concatenate(token_adv, axis=0)
    valid = jnp.concatenate(valid, axis=0)
    count1 = count[:, 0:1]

    def onward(owner):
        send(half(owner, c), half(owner, c), ag_c, (owner,), core_dev)

    for j in range(1, fi):
        owner = o * fi + lax.rem(i + fi - j, fi)
        arrive(half(owner, c), ag_i, (0, j), inner_dev(j))
        onward(owner)
    for k in (1, 3, 2):
        o_from = lax.rem(o + FO - k, FO)
        owner = o_from * fi + i
        arrive(half(owner, c), ag_o, (k,), outer_dev(k))
        for j in range(1, fi):
            send(half(owner, c), half(owner, c), ag_i, (k, j), inner_dev(j))
        onward(owner)
    for k in (1, 3, 2):
        o_from = lax.rem(o + FO - k, FO)
        for j in range(1, fi):
            owner = o_from * fi + lax.rem(i + fi - j, fi)
            arrive(half(owner, c), ag_i, (k, j), inner_dev(j))
            onward(owner)

    def forward(qq, carry):
        ssq, shv = carry
        span = pl.ds(pl.multiple_of(qq * cq, 128), cq)
        h = res[:, span].astype(F32) + jnp.dot(ctx[...], w[qq], preferred_element_type=F32)
        hid[qq] = h
        v = gain[:, span] * tgt[:, span].astype(F32)
        return (
            ssq + jnp.sum(h * h, axis=1, keepdims=True),
            shv + jnp.sum(h * v, axis=1, keepdims=True),
        )

    zero_t = jnp.zeros((tokens, 1), F32)
    sums = lax.fori_loop(2 * c, 2 * c + 2, forward, (zero_t, zero_t))
    for owner_k in range(1, fsdp_ways):
        owner = lax.rem(f + owner_k, fsdp_ways)
        arrive(half(owner, 1 - c), ag_c, (owner,), core_dev)
    sums = lax.fori_loop(2 - 2 * c, 4 - 2 * c, forward, sums)
    ssq, shv = sums
    rinv = lax.rsqrt(ssq / dw + 1e-06)
    score = shv * rinv
    ratio = jnp.exp(score - base)
    plain = ratio * token_adv
    clipped = jnp.clip(ratio, 0.8, 1.2) * token_adv
    loss_local = jnp.sum(valid * -jnp.minimum(plain, clipped), axis=0, keepdims=True)
    dscore = -valid * jnp.where(plain <= clipped, plain, 0.0) / count1
    lead = dscore * rinv * (32.0 * all_tokens * math.sqrt(dw))
    inner_scale = rinv * rinv * shv / dw

    def make_gh(qq):
        span = pl.ds(pl.multiple_of(qq * cq, 128), cq)
        v = gain[:, span] * tgt[:, span].astype(F32)
        ghs[qq] = (lead * (v - hid[qq] * inner_scale)).astype(BF16)

    for k in (2, 3, 1):
        there = lax.rem(q + k, Q)
        make_gh(there)
        send(ghs.at[there], ghr.at[q], gx, (k,), group_dev(k))
    make_gh(q)
    ghr[q] = ghs[q]
    ls[o, so, i, q] = jnp.broadcast_to(loss_local, (8, 128))
    for k in range(1, Q):
        mine = ls.at[o, so, i, q]
        send(mine, mine, ls1, (k,), group_dev(k))

    for k in range(1, Q):
        arrive(ctxt.at[lax.rem(q + Q - k, Q)], cx, (k,), group_dev(k))
    for k in range(1, Q):
        arrive(ghr.at[lax.rem(q + Q - k, Q)], gx, (k,), group_dev(k))

    def term(owner):
        total = jnp.dot(ctxt[0, rows_of(owner), :], ghr[0], preferred_element_type=F32)
        for a in range(1, Q):
            total += jnp.dot(ctxt[a, rows_of(owner), :], ghr[a], preferred_element_type=F32)
        return total

    order = (2, 1, 3, 0)
    for k in order:
        for j in range(1, fi):
            owner = lax.rem(o + k, FO) * fi + lax.rem(i + j, fi)
            dws[k, j - 1] = term(owner).astype(BF16)
            send(dws.at[k, j - 1], irecv.at[k, j - 1], rs_i, (k, j), inner_dev(j))

    @pl.loop(0, FO)
    def _(k):
        part[k] = term(lax.rem(o + k, FO) * fi + i)

    for k in range(1, Q):
        arrive(ls.at[o, so, i, lax.rem(q + Q - k, Q)], ls1, (k,), group_dev(k))
    for j in range(1, fi):
        mine = ls.at[o, so, i]
        send(mine, mine, ls2, (j,), inner_dev(j))

    for k in order:
        for j in range(1, fi):
            arrive(irecv.at[k, j - 1], rs_i, (k, j), inner_dev(j))
        total = part[k]
        for j in range(1, fi):
            total = total + irecv[k, j - 1].astype(F32)
        if k == 0:
            part[0] = total
        if k != 0 or so_ways > 1:
            obuf[k] = total.astype(BF16)
        for m in range(so_ways):
            if (m, k) != (0, 0):
                send(obuf.at[k], orecv.at[m, k], rs_o, (m, k), outer_dev(k, m))

    for j in range(1, fi):
        arrive(ls.at[o, so, lax.rem(i + fi - j, fi)], ls2, (j,), inner_dev(j))
    for m, k in outer:
        mine = ls.at[o, so]
        send(mine, mine, ls3, (m, k), outer_dev(k, m))

    @pl.loop(0, aw // 256)
    def _(t):
        span = pl.ds(pl.multiple_of(t * 256, 256), 256)
        total = lax.dot_general(
            ghs[0], w[0, span, :], (((1,), (1,)), ((), ())), preferred_element_type=F32
        )
        for a in range(1, Q):
            total += lax.dot_general(
                ghs[a], w[a, span, :], (((1,), (1,)), ((), ())), preferred_element_type=F32
            )
        gctx[:, span] = total.astype(BF16)

    for m, k in outer:
        arrive(orecv.at[m, k], rs_o, (m, k), outer_dev(k, m))
    total = part[0] if so_ways == 1 else obuf[0].astype(F32)
    for k in range(FO):
        both = None
        for m in range(so_ways):
            if (m, k) != (0, 0):
                one = orecv[m, k].astype(F32)
                both = one if both is None else both + one
        if both is not None:
            total = total + both
    scale = 1.0 / math.sqrt(all_tokens)
    fsend[...] = (total * scale).astype(BF16)
    for k in range(1, Q):
        send(fsend, frecv.at[k], fin, (k,), group_dev(k))
    gw[:, pl.ds(pl.multiple_of(q * cq, 128), cq)] = fsend[...].astype(F32)

    for m, k in outer:
        there = ls.at[lax.rem(o + FO - k, FO), lax.rem(so + so_ways - m, so_ways)]
        arrive(there, ls3, (m, k), outer_dev(k, m))
    loss_out[...] = jnp.sum(ls[...], axis=(0, 1, 2, 3)) / count1

    for k in range(1, Q):
        arrive(frecv.at[k], fin, (k,), group_dev(k))
        q_from = lax.rem(q + Q - k, Q)
        gw[:, pl.ds(pl.multiple_of(q_from * cq, 128), cq)] = frecv[k].astype(F32)
    for copy in sent:
        copy.wait_send()


def body(
    context,
    residual,
    target_rows,
    log_norm,
    norm_gain,
    out_proj,
    old_logprob,
    lengths,
    rewards,
    prompt_ids,
    placement,
):
    nrows, lmax, aw = context.shape
    dw = residual.shape[2]
    fsdp_ways = lax.axis_size("fsdp")
    seq_ways = lax.axis_size("seq")
    fi = fsdp_ways // FO
    so_ways = seq_ways // Q
    tokens = nrows * lmax
    blk = aw // fsdp_ways
    cq = dw // Q

    def spread(column):
        return jnp.broadcast_to(column.astype(F32).reshape(nrows, 1), (nrows, 128))

    packet = jnp.concatenate(
        [
            old_logprob,
            spread(rewards),
            spread(prompt_ids),
            spread(lengths),
            spread(placement),
            jnp.zeros((16 - 5 * nrows, 128), F32),
        ],
        axis=0,
    )
    vmem = pl.BlockSpec(memory_space=pltpu.VMEM)
    dma = pltpu.SemaphoreType.DMA
    gctx, gw, loss = pl.pallas_call(
        functools.partial(kernel, (fsdp_ways, seq_ways, nrows, lmax, dw, aw)),
        out_shape=(
            jax.ShapeDtypeStruct((tokens, aw), BF16),
            jax.ShapeDtypeStruct((blk, dw), F32),
            jax.ShapeDtypeStruct((8, 128), F32),
        ),
        in_specs=[vmem] * 7,
        out_specs=(vmem,) * 3,
        scratch_shapes=[
            pltpu.VMEM((Q, aw, cq), BF16),
            pltpu.VMEM((Q, aw, tokens), BF16),
            pltpu.VMEM((Q, tokens, cq), F32),
            pltpu.VMEM((Q, tokens, cq), BF16),
            pltpu.VMEM((Q, tokens, cq), BF16),
            pltpu.VMEM((FO, fi - 1, blk, cq), BF16),
            pltpu.VMEM((FO, fi - 1, blk, cq), BF16),
            pltpu.VMEM((FO, blk, cq), F32),
            pltpu.VMEM((FO, blk, cq), BF16),
            pltpu.VMEM((so_ways, FO, blk, cq), BF16),
            pltpu.VMEM((blk, cq), BF16),
            pltpu.VMEM((Q, blk, cq), BF16),
            pltpu.VMEM((FO, so_ways, fi, Q, 16, 128), F32),
            pltpu.VMEM((FO, so_ways, fi, Q, 8, 128), F32),
            dma((2, FO)),
            dma((2, FO, fi)),
            dma((2, fsdp_ways)),
            dma((2, Q)),
            dma((2, Q)),
            dma((2, FO, fi)),
            dma((2, so_ways, FO)),
            dma((2, Q)),
            dma((2, Q)),
            dma((2, fi)),
            dma((2, so_ways, FO)),
            dma((2, Q)),
            dma((2, fi)),
            dma((2, so_ways, FO)),
        ],
        compiler_params=pltpu.CompilerParams(
            collective_id=0, has_side_effects=True, vmem_limit_bytes=62 << 20
        ),
        cost_estimate=pl.CostEstimate(
            flops=6 * tokens * aw * dw, bytes_accessed=12 * tokens * dw, transcendentals=tokens
        ),
    )(
        context.reshape(tokens, aw),
        residual.reshape(tokens, dw),
        target_rows.reshape(tokens, dw),
        log_norm,
        norm_gain.reshape(1, dw),
        out_proj,
        packet,
    )
    return (gctx.reshape(nrows, lmax, aw), gw, loss[0, 0])


def solution(mesh):
    return jax.shard_map(
        body,
        mesh=mesh,
        in_specs=(
            P("fsdp", "seq", None),
            P("fsdp", "seq", None),
            P("fsdp", "seq", None),
            P("fsdp", "seq"),
            P(),
            P("fsdp", None),
            P("fsdp", "seq"),
            P("fsdp", "seq"),
            P("fsdp", "seq"),
            P("fsdp", "seq"),
            P("fsdp", "seq"),
        ),
        out_specs=(P("fsdp", "seq", None), P("fsdp", None), P()),
        check_vma=False,
    )
```

```python
import functools
import math

import jax
import jax.numpy as jnp
from jax import lax
from jax.experimental import pallas as pl
from jax.experimental.pallas import tpu as pltpu
from jax.sharding import PartitionSpec as P

GS = 16
FO = 4
Q = 4
EXTRA = 256
MESH = pl.DeviceIdType.MESH
F32 = jnp.float32
BF16 = jnp.bfloat16


def kernel(
    dims,
    ctx,
    res,
    tgt,
    lognorm,
    gain,
    wown,
    packet,
    gctx,
    gw,
    loss_out,
    w,
    ctxt,
    hid,
    ghs,
    ghr,
    dws,
    irecv,
    part,
    obuf,
    orecv,
    fsend,
    frecv,
    pk,
    ls,
    ag_o,
    ag_i,
    ag_y,
    ag_c,
    cx,
    gx,
    rs_i,
    rs_o,
    fin,
    pk1,
    pk2,
    pk3,
    ls1,
    ls2,
    ls3,
):
    fsdp_ways, seq_ways, nrows, lmax, dw, aw = dims
    fi = fsdp_ways // FO
    so_ways = seq_ways // Q
    tokens = nrows * lmax
    blk = aw // fsdp_ways
    cq = dw // Q
    extra = EXTRA
    prompts = nrows * fsdp_ways * seq_ways // GS
    prows = max(8, prompts)
    all_tokens = tokens * fsdp_ways * seq_ways
    f = lax.axis_index("fsdp")
    s = lax.axis_index("seq")
    o = f // fi
    i = lax.rem(f, fi)
    so = s // Q
    q = lax.rem(s, Q)
    c = lax.rem(q, 2)

    def outer_dev(k, m=0):
        return (lax.rem(o + k, FO) * fi + i, lax.rem(so + m, so_ways) * Q + q)

    def inner_dev(j):
        return (o * fi + lax.rem(i + j, fi), s)

    def group_dev(k):
        return (f, so * Q + lax.rem(q + k, Q))

    q_core = q + 1 - 2 * c
    q_far = lax.rem(q + 2, Q)
    q_diag = lax.rem(q_core + 2, Q)
    core_dev = (f, so * Q + q_core)
    far_dev = (f, so * Q + q_far)
    outer = [(m, k) for k in range(FO) for m in range(so_ways) if (m, k) != (0, 0)]
    barrier = pltpu.get_barrier_semaphore()
    peers = [outer_dev(k, m) for m, k in outer]
    peers += [inner_dev(j) for j in range(1, fi)]
    peers += [group_dev(k) for k in range(1, Q)]
    for peer in peers:
        pl.semaphore_signal(barrier, inc=1, device_id=peer, device_id_type=MESH)
    pl.semaphore_wait(barrier, len(peers))

    sent = []
    ring = (1, 3, 2)

    def send(src, dst, sems, index, dev):
        copy = pltpu.make_async_remote_copy(
            src_ref=src,
            dst_ref=dst,
            send_sem=sems.at[(0,) + index],
            recv_sem=sems.at[(1,) + index],
            device_id=dev,
            device_id_type=MESH,
        )
        copy.start()
        sent.append(copy)

    def arrive(dst, sems, index, dev):
        pltpu.make_async_remote_copy(
            src_ref=dst,
            dst_ref=dst,
            send_sem=sems.at[(0,) + index],
            recv_sem=sems.at[(1,) + index],
            device_id=dev,
            device_id_type=MESH,
        ).wait_recv()

    def rows_of(owner):
        return pl.ds(pl.multiple_of(owner * blk, blk), blk)

    def piece(owner, quarter, kind):
        if kind == 0:
            return w.at[quarter, rows_of(owner), :]
        if kind == 1:
            return w.at[quarter, rows_of(owner), pl.ds(0, extra)]
        return w.at[quarter, rows_of(owner), pl.ds(extra, cq - extra)]

    def mine_at(owner, kind):
        return piece(owner, q if kind == 0 else q_far, kind)

    def cores_at(owner, kind):
        return piece(owner, q_core if kind == 0 else q_diag, kind)

    pk[o, so, i, q] = packet[...]
    for k in range(1, Q):
        mine = pk.at[o, so, i, q]
        send(mine, mine, pk1, (k,), group_dev(k))

    for part_q in range(Q):
        w[part_q, rows_of(f), :] = wown[:, part_q * cq : (part_q + 1) * cq]
    for j in range(1, fi):
        for kind in (0, 1):
            send(mine_at(f, kind), mine_at(f, kind), ag_i, (kind, 0, j), inner_dev(j))
    for k in ring:
        for kind in (0, 1):
            send(mine_at(f, kind), mine_at(f, kind), ag_o, (kind, k), outer_dev(k))

    @pl.loop(0, aw // 256)
    def _(t):
        span = pl.ds(pl.multiple_of(t * 256, 256), 256)
        ctxt[q, span, :] = ctx[:, span].T

    send(ctxt.at[q], ctxt.at[q], cx, (1,), far_dev)
    send(ctxt.at[q], ctxt.at[q], cx, (2,), core_dev)

    for k in range(1, Q):
        there = pk.at[o, so, i, lax.rem(q + Q - k, Q)]
        arrive(there, pk1, (k,), group_dev(k))
    for j in range(1, fi):
        mine = pk.at[o, so, i]
        send(mine, mine, pk2, (j,), inner_dev(j))
    for j in range(1, fi):
        there = pk.at[o, so, lax.rem(i + fi - j, fi)]
        arrive(there, pk2, (j,), inner_dev(j))
    for m, k in outer:
        mine = pk.at[o, so]
        send(mine, mine, pk3, (m, k), outer_dev(k, m))
    for m, k in outer:
        there = pk.at[lax.rem(o + FO - k, FO), lax.rem(so + so_ways - m, so_ways)]
        arrive(there, pk3, (m, k), outer_dev(k, m))

    prompt_row = lax.broadcasted_iota(jnp.int32, (prows, 128), 0).astype(F32)
    zero_p = jnp.zeros((prows, 128), F32)
    zero_r = jnp.zeros((1, 128), F32)

    def over_devices(fa, carry):
        for sa in range(seq_ways):
            at = (fa // fi, sa // Q, lax.rem(fa, fi), sa % Q)
            for r in range(nrows):
                gsum, gsq, count = carry
                reward = pk[at + (pl.ds(nrows + r, 1), slice(None))]
                prompt = pk[at + (pl.ds(2 * nrows + r, 1), slice(None))]
                length = pk[at + (pl.ds(3 * nrows + r, 1), slice(None))]
                hot = prompt == prompt_row
                gsum = gsum + jnp.where(hot, reward, 0.0)
                gsq = gsq + jnp.where(hot, reward * reward, 0.0)
                carry = (gsum, gsq, count + length)
        return carry

    gsum, gsq, count = lax.fori_loop(0, fsdp_ways, over_devices, (zero_p, zero_p, zero_r))
    gmean = gsum / GS
    gvar = gsq / GS - gmean * gmean

    def over_column(fa, carry):
        at = (fa // fi, so, lax.rem(fa, fi), q)
        for r in range(nrows):
            old = pk[at + (pl.ds(r, 1), slice(None))]
            reward = pk[at + (pl.ds(nrows + r, 1), slice(None))]
            prompt = pk[at + (pl.ds(2 * nrows + r, 1), slice(None))]
            length = pk[at + (pl.ds(3 * nrows + r, 1), slice(None))]
            dest = pk[at + (pl.ds(4 * nrows + r, 1), slice(None))]
            hot = prompt == prompt_row
            mean = jnp.sum(jnp.where(hot, gmean, 0.0), axis=0, keepdims=True)
            var = jnp.sum(jnp.where(hot, gvar, 0.0), axis=0, keepdims=True)
            adv = (reward - mean) / jnp.sqrt(var + 0.25)
            fresh = []
            for j in range(nrows):
                chosen = dest == (f * nrows + j).astype(F32)
                l_old, l_adv, l_len = carry[3 * j : 3 * j + 3]
                fresh += [
                    l_old + jnp.where(chosen, old, 0.0),
                    l_adv + jnp.where(chosen, adv, 0.0),
                    l_len + jnp.where(chosen, length, 0.0),
                ]
            carry = tuple(fresh)
        return carry

    learned = lax.fori_loop(0, fsdp_ways, over_column, (zero_r,) * (3 * nrows))
    eye_r = lax.broadcasted_iota(jnp.int32, (lmax, lmax), 0)
    eye_c = lax.broadcasted_iota(jnp.int32, (lmax, lmax), 1)
    offset = lax.broadcasted_iota(jnp.int32, (lmax, 1), 0).astype(F32)

    def upright(row):
        spread = jnp.broadcast_to(row, (lmax, lmax))
        return jnp.sum(jnp.where(eye_r == eye_c, spread, 0.0), axis=1, keepdims=True)

    base, token_adv, valid = [], [], []
    for j in range(nrows):
        l_old, l_adv, l_len = learned[3 * j : 3 * j + 3]
        base.append(upright(lognorm[pl.ds(j, 1), :]) + upright(l_old))
        token_adv.append(jnp.broadcast_to(l_adv[:, 0:1], (lmax, 1)))
        valid.append((offset < l_len[:, 0:1]).astype(F32))
    base = jnp.concatenate(base, axis=0)
    token_adv = jnp.concatenate(token_adv, axis=0)
    valid = jnp.concatenate(valid, axis=0)
    count1 = count[:, 0:1]

    def onward(owner, kind):
        if kind == 0:
            there = piece(owner, q, 2)
            send(there, there, ag_y, (owner,), far_dev)
        send(mine_at(owner, kind), mine_at(owner, kind), ag_c, (kind, owner), core_dev)

    for j in range(1, fi):
        owner = o * fi + lax.rem(i + fi - j, fi)
        for kind in (0, 1):
            arrive(mine_at(owner, kind), ag_i, (kind, 0, j), inner_dev(j))
            onward(owner, kind)
    for k in ring:
        owner = lax.rem(o + FO - k, FO) * fi + i
        for kind in (0, 1):
            here = mine_at(owner, kind)
            arrive(here, ag_o, (kind, k), outer_dev(k))
            for j in range(1, fi):
                send(here, here, ag_i, (kind, k, j), inner_dev(j))
            onward(owner, kind)
    for k in ring:
        for j in range(1, fi):
            owner = lax.rem(o + FO - k, FO) * fi + lax.rem(i + fi - j, fi)
            for kind in (0, 1):
                arrive(mine_at(owner, kind), ag_i, (kind, k, j), inner_dev(j))
                onward(owner, kind)

    def forward(qq, carry):
        ssq, shv = carry
        span = pl.ds(pl.multiple_of(qq * cq, 128), cq)
        h = res[:, span].astype(F32) + jnp.dot(ctx[...], w[qq], preferred_element_type=F32)
        hid[qq] = h
        v = gain[:, span] * tgt[:, span].astype(F32)
        return (
            ssq + jnp.sum(h * h, axis=1, keepdims=True),
            shv + jnp.sum(h * v, axis=1, keepdims=True),
        )

    zero_t = jnp.zeros((tokens, 1), F32)
    sums = lax.fori_loop(q, q + 1, forward, (zero_t, zero_t))
    order = [(0, j) for j in range(1, fi)] + [(k, j) for k in ring for j in range(fi)]
    owners = [lax.rem(o + FO - k, FO) * fi + lax.rem(i + fi - j, fi) for k, j in order]
    for owner in owners:
        there = mine_at(owner, 2)
        arrive(there, ag_y, (owner,), far_dev)
        send(there, there, ag_c, (2, owner), core_dev)
    arrive(ctxt.at[q_far], cx, (1,), far_dev)
    send(ctxt.at[q_far], ctxt.at[q_far], cx, (3,), core_dev)
    sums = lax.fori_loop(q_far, q_far + 1, forward, sums)
    for owner in owners:
        for kind in (0, 1, 2):
            arrive(cores_at(owner, kind), ag_c, (kind, owner), core_dev)
    sums = lax.fori_loop(0, 2, lambda t, both: forward(lax.rem(q_core + 2 * t, Q), both), sums)
    ssq, shv = sums
    rinv = lax.rsqrt(ssq / dw + 1e-06)
    score = shv * rinv
    ratio = jnp.exp(score - base)
    plain = ratio * token_adv
    clipped = jnp.clip(ratio, 0.8, 1.2) * token_adv
    loss_local = jnp.sum(valid * -jnp.minimum(plain, clipped), axis=0, keepdims=True)
    dscore = -valid * jnp.where(plain <= clipped, plain, 0.0) / count1
    lead = dscore * rinv * (32.0 * all_tokens * math.sqrt(dw))
    inner_scale = rinv * rinv * shv / dw

    def make_gh(qq):
        span = pl.ds(pl.multiple_of(qq * cq, 128), cq)
        v = gain[:, span] * tgt[:, span].astype(F32)
        ghs[qq] = (lead * (v - hid[qq] * inner_scale)).astype(BF16)

    for k in (2, 3, 1):
        there = lax.rem(q + k, Q)
        make_gh(there)
        send(ghs.at[there], ghr.at[q], gx, (k,), group_dev(k))
    make_gh(q)
    ghr[q] = ghs[q]
    ls[o, so, i, q] = jnp.broadcast_to(loss_local, (8, 128))
    for k in range(1, Q):
        mine = ls.at[o, so, i, q]
        send(mine, mine, ls1, (k,), group_dev(k))

    arrive(ctxt.at[q_core], cx, (2,), core_dev)
    arrive(ctxt.at[q_diag], cx, (3,), core_dev)
    for k in range(1, Q):
        arrive(ghr.at[lax.rem(q + Q - k, Q)], gx, (k,), group_dev(k))

    def term(owner):
        total = jnp.dot(ctxt[0, rows_of(owner), :], ghr[0], preferred_element_type=F32)
        for a in range(1, Q):
            total += jnp.dot(ctxt[a, rows_of(owner), :], ghr[a], preferred_element_type=F32)
        return total

    order = (1, 3, 2, 0)
    for k in order:
        for j in range(1, fi):
            owner = lax.rem(o + k, FO) * fi + lax.rem(i + j, fi)
            dws[k, j - 1] = term(owner).astype(BF16)
            send(dws.at[k, j - 1], irecv.at[k, j - 1], rs_i, (k, j), inner_dev(j))

    @pl.loop(0, FO)
    def _(k):
        part[k] = term(lax.rem(o + k, FO) * fi + i)

    for k in range(1, Q):
        arrive(ls.at[o, so, i, lax.rem(q + Q - k, Q)], ls1, (k,), group_dev(k))
    for j in range(1, fi):
        mine = ls.at[o, so, i]
        send(mine, mine, ls2, (j,), inner_dev(j))

    for k in order:
        for j in range(1, fi):
            arrive(irecv.at[k, j - 1], rs_i, (k, j), inner_dev(j))
        total = part[k]
        for j in range(1, fi):
            total = total + irecv[k, j - 1].astype(F32)
        if k == 0:
            part[0] = total
        if k != 0 or so_ways > 1:
            obuf[k] = total.astype(BF16)
        for m in range(so_ways):
            if (m, k) != (0, 0):
                send(obuf.at[k], orecv.at[m, k], rs_o, (m, k), outer_dev(k, m))

    for j in range(1, fi):
        arrive(ls.at[o, so, lax.rem(i + fi - j, fi)], ls2, (j,), inner_dev(j))
    for m, k in outer:
        mine = ls.at[o, so]
        send(mine, mine, ls3, (m, k), outer_dev(k, m))

    @pl.loop(0, aw // 256)
    def _(t):
        span = pl.ds(pl.multiple_of(t * 256, 256), 256)
        total = lax.dot_general(
            ghs[0], w[0, span, :], (((1,), (1,)), ((), ())), preferred_element_type=F32
        )
        for a in range(1, Q):
            total += lax.dot_general(
                ghs[a], w[a, span, :], (((1,), (1,)), ((), ())), preferred_element_type=F32
            )
        gctx[:, span] = total.astype(BF16)

    for m, k in outer:
        arrive(orecv.at[m, k], rs_o, (m, k), outer_dev(k, m))
    total = part[0] if so_ways == 1 else obuf[0].astype(F32)
    for k in range(FO):
        both = None
        for m in range(so_ways):
            if (m, k) != (0, 0):
                one = orecv[m, k].astype(F32)
                both = one if both is None else both + one
        if both is not None:
            total = total + both
    scale = 1.0 / math.sqrt(all_tokens)
    fsend[...] = (total * scale).astype(BF16)
    send(fsend, frecv.at[1], fin, (1,), far_dev)
    send(fsend, frecv.at[2], fin, (2,), core_dev)
    gw[:, pl.ds(pl.multiple_of(q * cq, 128), cq)] = fsend[...].astype(F32)

    for m, k in outer:
        there = ls.at[lax.rem(o + FO - k, FO), lax.rem(so + so_ways - m, so_ways)]
        arrive(there, ls3, (m, k), outer_dev(k, m))
    loss_out[...] = jnp.sum(ls[...], axis=(0, 1, 2, 3)) / count1

    arrive(frecv.at[1], fin, (1,), far_dev)
    send(frecv.at[1], frecv.at[3], fin, (3,), core_dev)
    gw[:, pl.ds(pl.multiple_of(q_far * cq, 128), cq)] = frecv[1].astype(F32)
    arrive(frecv.at[2], fin, (2,), core_dev)
    gw[:, pl.ds(pl.multiple_of(q_core * cq, 128), cq)] = frecv[2].astype(F32)
    arrive(frecv.at[3], fin, (3,), core_dev)
    gw[:, pl.ds(pl.multiple_of(q_diag * cq, 128), cq)] = frecv[3].astype(F32)
    for copy in sent:
        copy.wait_send()


def body(
    context,
    residual,
    target_rows,
    log_norm,
    norm_gain,
    out_proj,
    old_logprob,
    lengths,
    rewards,
    prompt_ids,
    placement,
):
    nrows, lmax, aw = context.shape
    dw = residual.shape[2]
    fsdp_ways = lax.axis_size("fsdp")
    seq_ways = lax.axis_size("seq")
    fi = fsdp_ways // FO
    so_ways = seq_ways // Q
    tokens = nrows * lmax
    blk = aw // fsdp_ways
    cq = dw // Q

    def spread(column):
        return jnp.broadcast_to(column.astype(F32).reshape(nrows, 1), (nrows, 128))

    packet = jnp.concatenate(
        [
            old_logprob,
            spread(rewards),
            spread(prompt_ids),
            spread(lengths),
            spread(placement),
            jnp.zeros((16 - 5 * nrows, 128), F32),
        ],
        axis=0,
    )
    vmem = pl.BlockSpec(memory_space=pltpu.VMEM)
    dma = pltpu.SemaphoreType.DMA
    gctx, gw, loss = pl.pallas_call(
        functools.partial(kernel, (fsdp_ways, seq_ways, nrows, lmax, dw, aw)),
        out_shape=(
            jax.ShapeDtypeStruct((tokens, aw), BF16),
            jax.ShapeDtypeStruct((blk, dw), F32),
            jax.ShapeDtypeStruct((8, 128), F32),
        ),
        in_specs=[vmem] * 7,
        out_specs=(vmem,) * 3,
        scratch_shapes=[
            pltpu.VMEM((Q, aw, cq), BF16),
            pltpu.VMEM((Q, aw, tokens), BF16),
            pltpu.VMEM((Q, tokens, cq), F32),
            pltpu.VMEM((Q, tokens, cq), BF16),
            pltpu.VMEM((Q, tokens, cq), BF16),
            pltpu.VMEM((FO, fi - 1, blk, cq), BF16),
            pltpu.VMEM((FO, fi - 1, blk, cq), BF16),
            pltpu.VMEM((FO, blk, cq), F32),
            pltpu.VMEM((FO, blk, cq), BF16),
            pltpu.VMEM((so_ways, FO, blk, cq), BF16),
            pltpu.VMEM((blk, cq), BF16),
            pltpu.VMEM((Q, blk, cq), BF16),
            pltpu.VMEM((FO, so_ways, fi, Q, 16, 128), F32),
            pltpu.VMEM((FO, so_ways, fi, Q, 8, 128), F32),
            dma((2, 2, FO)),
            dma((2, 2, FO, fi)),
            dma((2, fsdp_ways)),
            dma((2, 3, fsdp_ways)),
            dma((2, Q)),
            dma((2, Q)),
            dma((2, FO, fi)),
            dma((2, so_ways, FO)),
            dma((2, Q)),
            dma((2, Q)),
            dma((2, fi)),
            dma((2, so_ways, FO)),
            dma((2, Q)),
            dma((2, fi)),
            dma((2, so_ways, FO)),
        ],
        compiler_params=pltpu.CompilerParams(
            collective_id=0, has_side_effects=True, vmem_limit_bytes=62 << 20
        ),
        cost_estimate=pl.CostEstimate(
            flops=6 * tokens * aw * dw, bytes_accessed=12 * tokens * dw, transcendentals=tokens
        ),
    )(
        context.reshape(tokens, aw),
        residual.reshape(tokens, dw),
        target_rows.reshape(tokens, dw),
        log_norm,
        norm_gain.reshape(1, dw),
        out_proj,
        packet,
    )
    return (gctx.reshape(nrows, lmax, aw), gw, loss[0, 0])


def solution(mesh):
    return jax.shard_map(
        body,
        mesh=mesh,
        in_specs=(
            P("fsdp", "seq", None),
            P("fsdp", "seq", None),
            P("fsdp", "seq", None),
            P("fsdp", "seq"),
            P(),
            P("fsdp", None),
            P("fsdp", "seq"),
            P("fsdp", "seq"),
            P("fsdp", "seq"),
            P("fsdp", "seq"),
            P("fsdp", "seq"),
        ),
        out_specs=(P("fsdp", "seq", None), P("fsdp", None), P()),
        check_vma=False,
    )
```

```python
import functools
import math

import jax
import jax.numpy as jnp
from jax import lax
from jax.experimental import pallas as pl
from jax.experimental.pallas import tpu as pltpu
from jax.sharding import PartitionSpec as P

GS = 16
FO = 4
Q = 4
EXTRA = 256
MESH = pl.DeviceIdType.MESH
F32 = jnp.float32
BF16 = jnp.bfloat16


def kernel(
    dims,
    ctx,
    res,
    tgt,
    lognorm,
    gain1,
    wown,
    old,
    rewards,
    prompt_ids,
    lengths,
    placement,
    gctx,
    gw,
    loss_out,
    w,
    ctxt,
    hid,
    ghs,
    ghr,
    dws,
    irecv,
    part,
    obuf,
    orecv,
    fsend,
    frecv,
    pk,
    ls,
    ag_o,
    ag_i,
    ag_y,
    ag_c,
    cx,
    gx,
    rs_i,
    rs_o,
    fin,
    pk1,
    pk2,
    pk3,
    ls1,
    ls2,
    ls3,
    gain,
):
    fsdp_ways, seq_ways, nrows, lmax, dw, aw = dims
    fi = fsdp_ways // FO
    so_ways = seq_ways // Q
    tokens = nrows * lmax
    blk = aw // fsdp_ways
    cq = dw // Q
    extra = EXTRA
    prompts = nrows * fsdp_ways * seq_ways // GS
    prows = max(8, prompts)
    all_tokens = tokens * fsdp_ways * seq_ways
    f = lax.axis_index("fsdp")
    s = lax.axis_index("seq")
    o = f // fi
    i = lax.rem(f, fi)
    so = s // Q
    q = lax.rem(s, Q)
    c = lax.rem(q, 2)

    def outer_dev(k, m=0):
        return (lax.rem(o + k, FO) * fi + i, lax.rem(so + m, so_ways) * Q + q)

    def inner_dev(j):
        return (o * fi + lax.rem(i + j, fi), s)

    def group_dev(k):
        return (f, so * Q + lax.rem(q + k, Q))

    q_core = q + 1 - 2 * c
    q_far = lax.rem(q + 2, Q)
    q_diag = lax.rem(q_core + 2, Q)
    core_dev = (f, so * Q + q_core)
    far_dev = (f, so * Q + q_far)
    outer = [(m, k) for k in range(FO) for m in range(so_ways) if (m, k) != (0, 0)]
    barrier = pltpu.get_barrier_semaphore()
    peers = [outer_dev(k, m) for m, k in outer]
    peers += [inner_dev(j) for j in range(1, fi)]
    peers += [group_dev(k) for k in range(1, Q)]
    for peer in peers:
        pl.semaphore_signal(barrier, inc=1, device_id=peer, device_id_type=MESH)
    pl.semaphore_wait(barrier, len(peers))

    sent = []
    ring = (1, 3, 2)

    def send(src, dst, sems, index, dev):
        copy = pltpu.make_async_remote_copy(
            src_ref=src,
            dst_ref=dst,
            send_sem=sems.at[(0,) + index],
            recv_sem=sems.at[(1,) + index],
            device_id=dev,
            device_id_type=MESH,
        )
        copy.start()
        sent.append(copy)

    def arrive(dst, sems, index, dev):
        pltpu.make_async_remote_copy(
            src_ref=dst,
            dst_ref=dst,
            send_sem=sems.at[(0,) + index],
            recv_sem=sems.at[(1,) + index],
            device_id=dev,
            device_id_type=MESH,
        ).wait_recv()

    def rows_of(owner):
        return pl.ds(pl.multiple_of(owner * blk, blk), blk)

    def piece(owner, quarter, kind):
        if kind == 0:
            return w.at[quarter, rows_of(owner), :]
        if kind == 1:
            return w.at[quarter, rows_of(owner), pl.ds(0, extra)]
        return w.at[quarter, rows_of(owner), pl.ds(extra, cq - extra)]

    def mine_at(owner, kind):
        return piece(owner, q if kind == 0 else q_far, kind)

    def cores_at(owner, kind):
        return piece(owner, q_core if kind == 0 else q_diag, kind)

    at_home = (o, so, i, q)
    pk[at_home] = jnp.zeros((16, 128), F32)
    pk[at_home + (pl.ds(0, nrows), slice(None))] = old[...]
    for n, field in enumerate((rewards, prompt_ids, lengths, placement)):
        for r in range(nrows):
            pk[at_home + (pl.ds((n + 1) * nrows + r, 1), slice(None))] = jnp.broadcast_to(
                field[:, r : r + 1].astype(F32), (1, 128)
            )
    for k in range(1, Q):
        mine = pk.at[o, so, i, q]
        send(mine, mine, pk1, (k,), group_dev(k))

    gain[...] = gain1[...].reshape(1, dw)

    for part_q in range(Q):
        w[part_q, rows_of(f), :] = wown[:, part_q * cq : (part_q + 1) * cq]
    for j in range(1, fi):
        for kind in (0, 1):
            send(mine_at(f, kind), mine_at(f, kind), ag_i, (kind, 0, j), inner_dev(j))
    for k in ring:
        for kind in (0, 1):
            send(mine_at(f, kind), mine_at(f, kind), ag_o, (kind, k), outer_dev(k))

    @pl.loop(0, aw // 256)
    def _(t):
        span = pl.ds(pl.multiple_of(t * 256, 256), 256)
        ctxt[q, span, :] = ctx[:, span].T

    send(ctxt.at[q], ctxt.at[q], cx, (1,), far_dev)
    send(ctxt.at[q], ctxt.at[q], cx, (2,), core_dev)

    def onward(owner, kind):
        if kind == 0:
            there = piece(owner, q, 2)
            send(there, there, ag_y, (owner,), far_dev)
        send(mine_at(owner, kind), mine_at(owner, kind), ag_c, (kind, owner), core_dev)

    for j in range(1, fi):
        owner = o * fi + lax.rem(i + fi - j, fi)
        for kind in (0, 1):
            arrive(mine_at(owner, kind), ag_i, (kind, 0, j), inner_dev(j))
            onward(owner, kind)
    for k in range(1, Q):
        there = pk.at[o, so, i, lax.rem(q + Q - k, Q)]
        arrive(there, pk1, (k,), group_dev(k))
    for j in range(1, fi):
        mine = pk.at[o, so, i]
        send(mine, mine, pk2, (j,), inner_dev(j))
    for k in ring:
        owner = lax.rem(o + FO - k, FO) * fi + i
        for kind in (0, 1):
            here = mine_at(owner, kind)
            arrive(here, ag_o, (kind, k), outer_dev(k))
            for j in range(1, fi):
                send(here, here, ag_i, (kind, k, j), inner_dev(j))
            onward(owner, kind)
    for j in range(1, fi):
        there = pk.at[o, so, lax.rem(i + fi - j, fi)]
        arrive(there, pk2, (j,), inner_dev(j))
    for m, k in outer:
        mine = pk.at[o, so]
        send(mine, mine, pk3, (m, k), outer_dev(k, m))
    for k in ring:
        for j in range(1, fi):
            owner = lax.rem(o + FO - k, FO) * fi + lax.rem(i + fi - j, fi)
            for kind in (0, 1):
                arrive(mine_at(owner, kind), ag_i, (kind, k, j), inner_dev(j))
                onward(owner, kind)

    for m, k in outer:
        there = pk.at[lax.rem(o + FO - k, FO), lax.rem(so + so_ways - m, so_ways)]
        arrive(there, pk3, (m, k), outer_dev(k, m))

    prompt_row = lax.broadcasted_iota(jnp.int32, (prows, 128), 0).astype(F32)
    zero_p = jnp.zeros((prows, 128), F32)
    zero_r = jnp.zeros((1, 128), F32)

    def over_devices(fa, carry):
        for sa in range(seq_ways):
            at = (fa // fi, sa // Q, lax.rem(fa, fi), sa % Q)
            for r in range(nrows):
                gsum, gsq, count = carry
                reward = pk[at + (pl.ds(nrows + r, 1), slice(None))]
                prompt = pk[at + (pl.ds(2 * nrows + r, 1), slice(None))]
                length = pk[at + (pl.ds(3 * nrows + r, 1), slice(None))]
                hot = prompt == prompt_row
                gsum = gsum + jnp.where(hot, reward, 0.0)
                gsq = gsq + jnp.where(hot, reward * reward, 0.0)
                carry = (gsum, gsq, count + length)
        return carry

    gsum, gsq, count = lax.fori_loop(0, fsdp_ways, over_devices, (zero_p, zero_p, zero_r))
    gmean = gsum / GS
    gvar = gsq / GS - gmean * gmean

    def over_column(fa, carry):
        at = (fa // fi, so, lax.rem(fa, fi), q)
        for r in range(nrows):
            old = pk[at + (pl.ds(r, 1), slice(None))]
            reward = pk[at + (pl.ds(nrows + r, 1), slice(None))]
            prompt = pk[at + (pl.ds(2 * nrows + r, 1), slice(None))]
            length = pk[at + (pl.ds(3 * nrows + r, 1), slice(None))]
            dest = pk[at + (pl.ds(4 * nrows + r, 1), slice(None))]
            hot = prompt == prompt_row
            mean = jnp.sum(jnp.where(hot, gmean, 0.0), axis=0, keepdims=True)
            var = jnp.sum(jnp.where(hot, gvar, 0.0), axis=0, keepdims=True)
            adv = (reward - mean) / jnp.sqrt(var + 0.25)
            fresh = []
            for j in range(nrows):
                chosen = dest == (f * nrows + j).astype(F32)
                l_old, l_adv, l_len = carry[3 * j : 3 * j + 3]
                fresh += [
                    l_old + jnp.where(chosen, old, 0.0),
                    l_adv + jnp.where(chosen, adv, 0.0),
                    l_len + jnp.where(chosen, length, 0.0),
                ]
            carry = tuple(fresh)
        return carry

    learned = lax.fori_loop(0, fsdp_ways, over_column, (zero_r,) * (3 * nrows))
    eye_r = lax.broadcasted_iota(jnp.int32, (lmax, lmax), 0)
    eye_c = lax.broadcasted_iota(jnp.int32, (lmax, lmax), 1)
    offset = lax.broadcasted_iota(jnp.int32, (lmax, 1), 0).astype(F32)

    def upright(row):
        spread = jnp.broadcast_to(row, (lmax, lmax))
        return jnp.sum(jnp.where(eye_r == eye_c, spread, 0.0), axis=1, keepdims=True)

    base, token_adv, valid = [], [], []
    for j in range(nrows):
        l_old, l_adv, l_len = learned[3 * j : 3 * j + 3]
        base.append(upright(lognorm[pl.ds(j, 1), :]) + upright(l_old))
        token_adv.append(jnp.broadcast_to(l_adv[:, 0:1], (lmax, 1)))
        valid.append((offset < l_len[:, 0:1]).astype(F32))
    base = jnp.concatenate(base, axis=0)
    token_adv = jnp.concatenate(token_adv, axis=0)
    valid = jnp.concatenate(valid, axis=0)
    count1 = count[:, 0:1]

    def forward(qq, carry):
        ssq, shv = carry
        span = pl.ds(pl.multiple_of(qq * cq, 128), cq)
        h = res[:, span].astype(F32) + jnp.dot(ctx[...], w[qq], preferred_element_type=F32)
        hid[qq] = h
        v = gain[:, span] * tgt[:, span].astype(F32)
        return (
            ssq + jnp.sum(h * h, axis=1, keepdims=True),
            shv + jnp.sum(h * v, axis=1, keepdims=True),
        )

    zero_t = jnp.zeros((tokens, 1), F32)
    sums = lax.fori_loop(q, q + 1, forward, (zero_t, zero_t))
    order = [(0, j) for j in range(1, fi)] + [(k, j) for k in ring for j in range(fi)]
    owners = [lax.rem(o + FO - k, FO) * fi + lax.rem(i + fi - j, fi) for k, j in order]
    for owner in owners:
        there = mine_at(owner, 2)
        arrive(there, ag_y, (owner,), far_dev)
        send(there, there, ag_c, (2, owner), core_dev)
    arrive(ctxt.at[q_far], cx, (1,), far_dev)
    send(ctxt.at[q_far], ctxt.at[q_far], cx, (3,), core_dev)
    sums = lax.fori_loop(q_far, q_far + 1, forward, sums)
    for owner in owners:
        for kind in (0, 1, 2):
            arrive(cores_at(owner, kind), ag_c, (kind, owner), core_dev)
    sums = lax.fori_loop(0, 2, lambda t, both: forward(lax.rem(q_core + 2 * t, Q), both), sums)
    ssq, shv = sums
    rinv = lax.rsqrt(ssq / dw + 1e-06)
    score = shv * rinv
    ratio = jnp.exp(score - base)
    plain = ratio * token_adv
    clipped = jnp.clip(ratio, 0.8, 1.2) * token_adv
    loss_local = jnp.sum(valid * -jnp.minimum(plain, clipped), axis=0, keepdims=True)
    dscore = -valid * jnp.where(plain <= clipped, plain, 0.0) / count1
    lead = dscore * rinv * (32.0 * all_tokens * math.sqrt(dw))
    inner_scale = rinv * rinv * shv / dw

    def make_gh(qq):
        span = pl.ds(pl.multiple_of(qq * cq, 128), cq)
        v = gain[:, span] * tgt[:, span].astype(F32)
        ghs[qq] = (lead * (v - hid[qq] * inner_scale)).astype(BF16)

    for k in (2, 3, 1):
        there = lax.rem(q + k, Q)
        make_gh(there)
        send(ghs.at[there], ghr.at[q], gx, (k,), group_dev(k))
    make_gh(q)
    ghr[q] = ghs[q]
    ls[o, so, i, q] = jnp.broadcast_to(loss_local, (8, 128))
    for k in range(1, Q):
        mine = ls.at[o, so, i, q]
        send(mine, mine, ls1, (k,), group_dev(k))

    arrive(ctxt.at[q_core], cx, (2,), core_dev)
    arrive(ctxt.at[q_diag], cx, (3,), core_dev)
    for k in range(1, Q):
        arrive(ghr.at[lax.rem(q + Q - k, Q)], gx, (k,), group_dev(k))

    def term(owner):
        total = jnp.dot(ctxt[0, rows_of(owner), :], ghr[0], preferred_element_type=F32)
        for a in range(1, Q):
            total += jnp.dot(ctxt[a, rows_of(owner), :], ghr[a], preferred_element_type=F32)
        return total

    order = (1, 3, 2, 0)
    for k in order:
        for j in range(1, fi):
            owner = lax.rem(o + k, FO) * fi + lax.rem(i + j, fi)
            dws[k, j - 1] = term(owner).astype(BF16)
            send(dws.at[k, j - 1], irecv.at[k, j - 1], rs_i, (k, j), inner_dev(j))

    @pl.loop(0, FO)
    def _(k):
        part[k] = term(lax.rem(o + k, FO) * fi + i)

    for k in range(1, Q):
        arrive(ls.at[o, so, i, lax.rem(q + Q - k, Q)], ls1, (k,), group_dev(k))
    for j in range(1, fi):
        mine = ls.at[o, so, i]
        send(mine, mine, ls2, (j,), inner_dev(j))

    for k in order:
        for j in range(1, fi):
            arrive(irecv.at[k, j - 1], rs_i, (k, j), inner_dev(j))
        total = part[k]
        for j in range(1, fi):
            total = total + irecv[k, j - 1].astype(F32)
        if k == 0:
            part[0] = total
        if k != 0 or so_ways > 1:
            obuf[k] = total.astype(BF16)
        for m in range(so_ways):
            if (m, k) != (0, 0):
                send(obuf.at[k], orecv.at[m, k], rs_o, (m, k), outer_dev(k, m))

    for j in range(1, fi):
        arrive(ls.at[o, so, lax.rem(i + fi - j, fi)], ls2, (j,), inner_dev(j))
    for m, k in outer:
        mine = ls.at[o, so]
        send(mine, mine, ls3, (m, k), outer_dev(k, m))

    @pl.loop(0, aw // 256)
    def _(t):
        span = pl.ds(pl.multiple_of(t * 256, 256), 256)
        total = lax.dot_general(
            ghs[0], w[0, span, :], (((1,), (1,)), ((), ())), preferred_element_type=F32
        )
        for a in range(1, Q):
            total += lax.dot_general(
                ghs[a], w[a, span, :], (((1,), (1,)), ((), ())), preferred_element_type=F32
            )
        gctx[:, span] = total.astype(BF16)

    for m, k in outer:
        arrive(orecv.at[m, k], rs_o, (m, k), outer_dev(k, m))
    total = part[0] if so_ways == 1 else obuf[0].astype(F32)
    for k in range(FO):
        both = None
        for m in range(so_ways):
            if (m, k) != (0, 0):
                one = orecv[m, k].astype(F32)
                both = one if both is None else both + one
        if both is not None:
            total = total + both
    scale = 1.0 / math.sqrt(all_tokens)
    fsend[...] = (total * scale).astype(BF16)
    send(fsend, frecv.at[1], fin, (1,), far_dev)
    send(fsend, frecv.at[2], fin, (2,), core_dev)
    gw[:, pl.ds(pl.multiple_of(q * cq, 128), cq)] = fsend[...]

    for m, k in outer:
        there = ls.at[lax.rem(o + FO - k, FO), lax.rem(so + so_ways - m, so_ways)]
        arrive(there, ls3, (m, k), outer_dev(k, m))
    loss_out[...] = jnp.sum(ls[...], axis=(0, 1, 2, 3))[0:1, 0:1] / count1

    arrive(frecv.at[1], fin, (1,), far_dev)
    send(frecv.at[1], frecv.at[3], fin, (3,), core_dev)
    gw[:, pl.ds(pl.multiple_of(q_far * cq, 128), cq)] = frecv[1]
    arrive(frecv.at[2], fin, (2,), core_dev)
    gw[:, pl.ds(pl.multiple_of(q_core * cq, 128), cq)] = frecv[2]
    arrive(frecv.at[3], fin, (3,), core_dev)
    gw[:, pl.ds(pl.multiple_of(q_diag * cq, 128), cq)] = frecv[3]
    for copy in sent:
        copy.wait_send()


def body(
    context,
    residual,
    target_rows,
    log_norm,
    norm_gain,
    out_proj,
    old_logprob,
    lengths,
    rewards,
    prompt_ids,
    placement,
):
    nrows, lmax, aw = context.shape
    dw = residual.shape[2]
    fsdp_ways = lax.axis_size("fsdp")
    seq_ways = lax.axis_size("seq")
    fi = fsdp_ways // FO
    so_ways = seq_ways // Q
    tokens = nrows * lmax
    blk = aw // fsdp_ways
    cq = dw // Q

    vmem = pl.BlockSpec(memory_space=pltpu.VMEM)
    dma = pltpu.SemaphoreType.DMA
    gctx, gw, loss = pl.pallas_call(
        functools.partial(kernel, (fsdp_ways, seq_ways, nrows, lmax, dw, aw)),
        out_shape=(
            jax.ShapeDtypeStruct((tokens, aw), BF16),
            jax.ShapeDtypeStruct((blk, dw), BF16),
            jax.ShapeDtypeStruct((1, 1), F32),
        ),
        in_specs=[vmem] * 11,
        out_specs=(vmem,) * 3,
        scratch_shapes=[
            pltpu.VMEM((Q, aw, cq), BF16),
            pltpu.VMEM((Q, aw, tokens), BF16),
            pltpu.VMEM((Q, tokens, cq), F32),
            pltpu.VMEM((Q, tokens, cq), BF16),
            pltpu.VMEM((Q, tokens, cq), BF16),
            pltpu.VMEM((FO, fi - 1, blk, cq), BF16),
            pltpu.VMEM((FO, fi - 1, blk, cq), BF16),
            pltpu.VMEM((FO, blk, cq), F32),
            pltpu.VMEM((FO, blk, cq), BF16),
            pltpu.VMEM((so_ways, FO, blk, cq), BF16),
            pltpu.VMEM((blk, cq), BF16),
            pltpu.VMEM((Q, blk, cq), BF16),
            pltpu.VMEM((FO, so_ways, fi, Q, 16, 128), F32),
            pltpu.VMEM((FO, so_ways, fi, Q, 8, 128), F32),
            dma((2, 2, FO)),
            dma((2, 2, FO, fi)),
            dma((2, fsdp_ways)),
            dma((2, 3, fsdp_ways)),
            dma((2, Q)),
            dma((2, Q)),
            dma((2, FO, fi)),
            dma((2, so_ways, FO)),
            dma((2, Q)),
            dma((2, Q)),
            dma((2, fi)),
            dma((2, so_ways, FO)),
            dma((2, Q)),
            dma((2, fi)),
            dma((2, so_ways, FO)),
            pltpu.VMEM((1, dw), F32),
        ],
        compiler_params=pltpu.CompilerParams(
            collective_id=0, has_side_effects=True, vmem_limit_bytes=62 << 20
        ),
        cost_estimate=pl.CostEstimate(
            flops=6 * tokens * aw * dw, bytes_accessed=12 * tokens * dw, transcendentals=tokens
        ),
    )(
        context.reshape(tokens, aw),
        residual.reshape(tokens, dw),
        target_rows.reshape(tokens, dw),
        log_norm,
        norm_gain,
        out_proj,
        old_logprob,
        rewards.reshape(1, nrows),
        prompt_ids.reshape(1, nrows),
        lengths.reshape(1, nrows),
        placement.reshape(1, nrows),
    )
    return (gctx.reshape(nrows, lmax, aw), gw.astype(F32), loss.reshape(()))


def solution(mesh):
    return jax.shard_map(
        body,
        mesh=mesh,
        in_specs=(
            P("fsdp", "seq", None),
            P("fsdp", "seq", None),
            P("fsdp", "seq", None),
            P("fsdp", "seq"),
            P(),
            P("fsdp", None),
            P("fsdp", "seq"),
            P("fsdp", "seq"),
            P("fsdp", "seq"),
            P("fsdp", "seq"),
            P("fsdp", "seq"),
        ),
        out_specs=(P("fsdp", "seq", None), P("fsdp", None), P()),
        check_vma=False,
    )
```
